128 devices in a mesh: bra: 16 (over z, y), ket: 8 (over x, core).
Axes of the slice: x: 4, y: 4, z: 4, core: 2. Of those that a mesh axis runs over, the one named last changes fastest.
Arguments:
- quartet_tasks: int32 [16, 8, 512, 4], P('bra', 'ket'), may hold values from 0 to 767, as said below
- factors: bfloat16 [768, 16, 128], replicated, may hold values from -4.5 to 4.5
- density: bfloat16 [768, 96, 8, 256], P('bra', None, 'ket'), may hold values from -6 to 6
Outputs:
- fock_matrix: float32 [768, 96, 8, 256], P('bra', None, 'ket')
The draws below stay inside these ranges and needn't reach their ends.
Inputs may be any that keep to these rules, and one draw needn't show every extreme that they name: `quartet_tasks`: entries are shell numbers. On the device with bra index b and ket index k, every task's i lies among b * 48 to (b + 1) * 48 - 1 and its d has d % 8 == k. Within each half of a device's task list (the first 256 tasks and the rest), the shells c and j of all its tasks name row blocks of one bra index at most 96 times and share one remainder mod 8 at most 80 times; both bounds are reached in each half of every device's list, by the same bra index and the same remainder in both halves.
All inputs are finite; a program needn't handle non-finite values.
Results may differ from the reference program's by a relative error of at most 0.0066.
Values may be sent and summed in bfloat16 or wider, within the bound.
No kernel may reach another device: no remote copies, remote signals or barrier semaphores. Data moves between devices by JAX's collectives and lax.ppermute only.
A program may use at most 64 MiB of HBM per device.

```python
import jax
import jax.numpy as jnp
from jax import lax

FUNCS = 16
RANK = 128
BLK = 6
TASKS = 512
KETS = 8
NBLK = 768
ROWB = 48
COLB = 96
HALFB = 96
HALFK = 80
N_BRA = 16
N_KET = 8


def owner_list(key, forced, count_of_owners, capacity, item_count):
    second_key, third_key = jax.random.split(key, 2)
    slot_ids = jnp.arange(count_of_owners * capacity, dtype=jnp.int32)
    shuffled = jax.random.permutation(second_key, count_of_owners * capacity).astype(jnp.int32)
    ranking = jnp.argsort(shuffled, stable=True).astype(jnp.int32)
    scores = jnp.where(slot_ids // capacity == forced, slot_ids - count_of_owners * capacity, ranking)
    chosen = jnp.argsort(scores, stable=True)[:item_count].astype(jnp.int32)
    owner_ids = chosen // capacity
    mixing = jax.random.permutation(third_key, item_count)
    return owner_ids[mixing]


def draw_quartet_tasks(key, part):

    def one_device(device):
        device_key = jax.random.fold_in(key, device)
        bra_index = device // N_KET
        ket_index = device % N_KET
        forced_bra = jax.random.randint(jax.random.fold_in(device_key, 60), (), 0, N_BRA)
        forced_ket = jax.random.randint(jax.random.fold_in(device_key, 70), (), 0, N_KET)
        bra_owners = jnp.concatenate([owner_list(jax.random.fold_in(device_key, 10 + portion), forced_bra, N_BRA, HALFB, TASKS) for portion in range(2)])
        ket_owners = jnp.concatenate([owner_list(jax.random.fold_in(device_key, 20 + portion), forced_ket, N_KET, HALFK, TASKS) for portion in range(2)])
        inner = jax.random.randint(jax.random.fold_in(device_key, 30), (2 * TASKS,), 0, BLK)
        shells = bra_owners * ROWB + inner * N_KET + ket_owners
        shell_i = bra_index * ROWB + jax.random.randint(jax.random.fold_in(device_key, 40), (TASKS,), 0, ROWB)
        shell_d = jax.random.randint(jax.random.fold_in(device_key, 50), (TASKS,), 0, COLB) * N_KET + ket_index
        paired = shells.reshape(TASKS, 2)
        return jnp.stack([shell_i, paired[:, 1], paired[:, 0], shell_d], axis=1).astype(jnp.int32)
    devices = jnp.arange(N_BRA * N_KET, dtype=jnp.int32)
    return jax.vmap(one_device)(devices).reshape(N_BRA, N_KET, TASKS, 4)


def steps_of(rng, extent, pieces, smallest, top_value):
    def one(axis_at, shards_of):
        heights = jax.random.uniform(jax.random.fold_in(jax.random.fold_in(rng, 6), axis_at), (shards_of,), jnp.float32, smallest / len(pieces), top_value / len(pieces))
        return jnp.repeat(jnp.exp(heights), extent[axis_at] // shards_of).reshape((-1,) + (1,) * (len(extent) - axis_at - 1))

    level = one(*pieces[0])
    for cut in pieces[1:]:
        level = level * one(*cut)
    return level


def centred(stream_key, shape, deviation, limit, pieces=(), held_as=jnp.bfloat16):
    factor_of = steps_of(stream_key, shape, pieces, -0.22, 0.18) if pieces else 1.0
    drawn = jax.random.normal(stream_key, shape, jnp.float32) * deviation * factor_of
    return jnp.minimum(jnp.maximum(drawn, -limit), limit).astype(held_as)


def setup_inputs(seed: int = 0) -> dict:
    seeds = jax.random.split(jax.random.key(seed), 4)
    return {
        "quartet_tasks": draw_quartet_tasks(jax.random.fold_in(seeds[3], 71), 0),
        "factors": centred(seeds[1], (NBLK, FUNCS, RANK), 0.75, 4.5),
        "density": centred(seeds[2], (NBLK, COLB, KETS, FUNCS * FUNCS), 1.0, 6.0, ((0, 16), (2, 8))),
    }


tile_scale = 0.0625

def pair_vectors(left_shell, right_shell):
    shell_count, basis_functions, terms = left_shell.shape
    joined = left_shell[:, :, None, :].astype(jnp.float32) * right_shell[:, None, :, :].astype(jnp.float32)
    return joined.reshape(shell_count, basis_functions * basis_functions, terms).astype(jnp.bfloat16)

def quartet_terms(factors, task_group, dens_cd, density_block_jd):
    group_member_count = task_group.shape[0]
    basis_functions = factors.shape[1]
    bra_vec = pair_vectors(factors[task_group[:, 0]], factors[task_group[:, 1]])
    ket_vec = pair_vectors(factors[task_group[:, 2]], factors[task_group[:, 3]])
    raw_products = jnp.einsum('tpr,tqr->tpq', bra_vec.astype(jnp.float32), ket_vec.astype(jnp.float32))
    integral_tile = (tile_scale * raw_products * lax.rsqrt(1.0 + raw_products * raw_products)).astype(jnp.bfloat16)
    coulomb = jnp.einsum('tpq,tq->tp', integral_tile.astype(jnp.float32), dens_cd.astype(jnp.float32))
    reshaped_tile = integral_tile.reshape(group_member_count, basis_functions, basis_functions, basis_functions, basis_functions).astype(jnp.float32)
    exchange_contribution = jnp.einsum('kwzmp,kzp->kwm', reshaped_tile, density_block_jd.reshape(group_member_count, basis_functions, basis_functions).astype(jnp.float32))
    return (coulomb, exchange_contribution.reshape(group_member_count, basis_functions * basis_functions))

def reference(quartet_tasks, factors, density):
    quartets = quartet_tasks.reshape(-1, 4)
    block_size = density.shape[3]

    def block_step(task_group):
        shell_j = task_group[:, 1]
        shell_c = task_group[:, 2]
        shell_d = task_group[:, 3]
        dens_cd = density[shell_c, shell_d // KETS, shell_d % KETS]
        density_block_jd = density[shell_j, shell_d // KETS, shell_d % KETS]
        return quartet_terms(factors, task_group, dens_cd, density_block_jd)
    coulomb, exchange_contribution = lax.map(block_step, quartets.reshape(-1, 32, 4))
    coulomb = coulomb.reshape(-1, block_size)
    exchange_contribution = exchange_contribution.reshape(-1, block_size)
    fock_matrix = jnp.zeros(density.shape, jnp.float32)
    fock_matrix = fock_matrix.at[quartets[:, 0], quartets[:, 1] // KETS, quartets[:, 1] % KETS].add(coulomb)
    fock_matrix = fock_matrix.at[quartets[:, 0], quartets[:, 2] // KETS, quartets[:, 2] % KETS].add(-0.5 * exchange_contribution)
    return fock_matrix
```

```python
import functools

import jax
import jax.numpy as jnp
import numpy as np
from jax import lax
from jax.experimental import pallas as pl
from jax.experimental.pallas import tpu as pltpu
from jax.sharding import PartitionSpec as P

F32, BF16, I32 = jnp.float32, jnp.bfloat16, jnp.int32
FUNCS, RANK, BSZ = 16, 128, 256
NBLK, ROWB, COLB = 768, 48, 96
NBRA, NKET, TASKS = 16, 8, 512
HALF, CAPB, CAPK = 256, 96, 80
OUTROWS = 96
GROUP = 16
NB = ROWB * COLB
VM = pl.BlockSpec(memory_space=pltpu.VMEM)
SM = pl.BlockSpec(memory_space=pltpu.SMEM)
PARAMS = pltpu.CompilerParams(vmem_limit_bytes=60 * 1024 * 1024)


def iota(shape, dim):
    return lax.broadcasted_iota(I32, shape, dim)


def nt_dot(a, b):
    return lax.dot_general(a, b, (((1,), (1,)), ((), ())), preferred_element_type=F32)


def ranks(owners, count, upper, carry):
    marks = (iota((count, HALF), 0) == owners).astype(F32)
    before = jnp.dot(marks.astype(BF16), upper, preferred_element_type=F32) + carry
    place = jnp.sum(before * marks, axis=0, keepdims=True).astype(I32)
    return marks, place, carry + jnp.sum(marks, axis=1, keepdims=True)


def table(marks, place, value, width):
    at = (iota((width, HALF), 0) == place).astype(BF16)
    high = (value // 64).astype(F32)
    low = (value % 64).astype(F32)
    return nt_dot((marks * high).astype(BF16), at), nt_dot((marks * low).astype(BF16), at)


def prep_kernel(tasks, ids, slots, oslots, places):
    upper = (iota((HALF, HALF), 0) < iota((HALF, HALF), 1)).astype(BF16)
    for h in range(2):
        i, j, c, d = (tasks[r : r + 1, h * HALF : (h + 1) * HALF] for r in range(4))
        carry = jnp.zeros((NBRA, 1), F32)
        high = low = 0.0
        for k, s in enumerate((c, j)):
            own = s // ROWB
            marks, place, carry = ranks(own, NBRA, upper, carry)
            slots[k : k + 1, h * HALF : (h + 1) * HALF] = own * CAPB + place
            a, b = table(marks, place, (s % ROWB) * COLB + d // NKET, 128)
            high, low = high + a, low + b
        got = (high * 64.0 + low).astype(I32)
        ids[:, h * 128 : (h + 1) * 128] = jnp.where(iota((NBRA, 128), 1) < CAPB, got, carry.astype(I32))
        carry = jnp.zeros((NKET, 1), F32)
        high = low = 0.0
        for k, s in enumerate((j, c)):
            own = s % NKET
            marks, place, carry = ranks(own, NKET, upper, carry)
            oslots[k : k + 1, h * HALF : (h + 1) * HALF] = own * CAPK + place
            a, b = table(marks, place, (i % ROWB) * COLB + s // NKET + 1, 128)
            high, low = high + a, low + b
        places[h, :, 0:128] = high
        places[h, :, 128:256] = low


def prep(tasks):
    return pl.pallas_call(
        prep_kernel,
        out_shape=(
            jax.ShapeDtypeStruct((NBRA, 256), I32),
            jax.ShapeDtypeStruct((2, TASKS), I32),
            jax.ShapeDtypeStruct((2, TASKS), I32),
            jax.ShapeDtypeStruct((2, NKET, 256), F32),
        ),
        in_specs=[VM],
        out_specs=(VM,) * 4,
        compiler_params=PARAMS,
    )(tasks)


def spread(src, dst, rows):
    def step(k, _):
        for u in range(4):
            r = pl.multiple_of(k * 64 + u * 16, 16)
            v = src[pl.ds(r, 16), :].astype(F32)
            dst[pl.ds(2 * r, 16, stride=2), :] = v[:, :128]
            dst[pl.ds(2 * r + 1, 16, stride=2), :] = v[:, 128:]
        return 0

    lax.fori_loop(0, rows // 64, step, 0)


def gather_kernel(half, ids, dens, out, wide, got):
    spread(dens, wide, NB)

    def source(s, _):
        count = ids[s, half * 128 + CAPB]

        def step(k, _):
            for u in range(8):
                p = k * 8 + u
                r = ids[s, half * 128 + p]
                got[pl.ds((s * CAPB + p) * 2, 2), :] = wide[pl.ds(r * 2, 2), :]
            return 0

        lax.fori_loop(0, (count + 7) // 8, step, 0)
        return 0

    lax.fori_loop(0, NBRA, source, 0)

    def pack(k, _):
        for u in range(4):
            r = pl.multiple_of(k * 64 + u * 16, 16)
            out[pl.ds(r, 16), 0:128] = got[pl.ds(2 * r, 16, stride=2), :].astype(BF16)
            out[pl.ds(r, 16), 128:256] = got[pl.ds(2 * r + 1, 16, stride=2), :].astype(BF16)
        return 0

    lax.fori_loop(0, NBRA * CAPB // 64, pack, 0)


def gather(half, ids, dens):
    return pl.pallas_call(
        functools.partial(gather_kernel, half),
        out_shape=jax.ShapeDtypeStruct((NBRA * CAPB, 256), BF16),
        in_specs=[SM, VM],
        out_specs=VM,
        scratch_shapes=[pltpu.VMEM((2 * NB, 128), F32), pltpu.VMEM((2 * NBRA * CAPB, 128), F32)],
        compiler_params=PARAMS,
    )(ids, dens)


def constants():
    r = np.arange(256)
    lane = np.arange(128)
    spread_b = r[:, None] // 16 == lane[None, :] % 16
    sum_f = np.arange(16)[:, None] == r[None, :] // 16
    sum_b = r[:, None] // 16 == r[None, :] // 16
    keep_f = np.arange(16)[:, None] == lane[None, :] % 16
    return [jnp.asarray(x, BF16) for x in (spread_b, sum_f, sum_b)] + [jnp.asarray(keep_f, F32)]


def eval_kernel(
    half, tasks, slots, oslots, fac, fetched, places, spread_b, sum_f, sum_b, keep_f, out,
    rows, wide, outw, cd, jd, dsp, part, fin,
):
    base = half * HALF

    def widen(k, _):
        for u in range(8):
            rows[pl.ds(pl.multiple_of((k * 8 + u) * 16, 16), 16), :] = fac[k * 8 + u].astype(F32)
        return 0

    lax.fori_loop(0, NBLK // 8, widen, 0)
    spread(fetched, wide, NBRA * CAPB)
    keep = keep_f[...]

    def pairs(x, y):
        fy = fac[y]
        return jnp.concatenate(
            [
                jnp.broadcast_to(rows[pl.ds(x * FUNCS + a, 1), :], (FUNCS, RANK)).astype(BF16) * fy
                for a in range(FUNCS)
            ],
            axis=0,
        )

    def group(g, _):
        for n in range(GROUP):
            t = base + g * GROUP + n
            cd[2 * n : 2 * n + 2, :] = wide[pl.ds(slots[0, t] * 2, 2), :]
            block = wide[pl.ds(slots[1, t] * 2, 2), :]
            jd[n * 16 : n * 16 + 16, 0:128] = (jnp.broadcast_to(block[0:1], (16, 128)) * keep).astype(BF16)
            jd[n * 16 : n * 16 + 16, 128:256] = (jnp.broadcast_to(block[1:2], (16, 128)) * keep).astype(BF16)
        dsp[...] = jnp.dot(jd[...], spread_b[...], preferred_element_type=F32).astype(BF16)
        dcd = jnp.concatenate([cd[pl.ds(0, 16, stride=2), :], cd[pl.ds(1, 16, stride=2), :]], axis=1).astype(BF16)
        acc = jnp.zeros((GROUP, BSZ), F32)
        for n in range(GROUP):
            t = base + g * GROUP + n
            bra = pairs(tasks[0, t], tasks[1, t])
            ket = pairs(tasks[2, t], tasks[3, t])
            raw = nt_dot(ket, bra).astype(BF16)
            tile = raw * lax.rsqrt(raw * raw + BF16(1.0))
            coul = jnp.dot(dcd, tile, preferred_element_type=F32)
            acc = jnp.where(iota((GROUP, BSZ), 0) == n, coul, acc)
            dd = dsp[n * 16 : n * 16 + 16, :]
            dd = jnp.concatenate([dd, dd], axis=1)
            prod = jnp.concatenate([tile[16 * e : 16 * e + 16, :] * dd for e in range(16)], axis=0)
            part[n * 16 : n * 16 + 16, :] = jnp.dot(sum_f[...], prod, preferred_element_type=F32).astype(BF16)
        full = jnp.dot(part[...], sum_b[...], preferred_element_type=F32)
        full = jnp.where((iota((256, 256), 0) % 16) == (iota((256, 256), 1) % 16), full, 0.0)
        exch = jnp.dot(sum_f[...], full.astype(BF16), preferred_element_type=F32) * (-0.5 * 0.0625)
        acc = acc * 0.0625
        for k, v in enumerate((acc, exch)):
            fin[pl.ds(32 * k, 16, stride=2), :] = v[:, :128]
            fin[pl.ds(32 * k + 1, 16, stride=2), :] = v[:, 128:]
        for n in range(GROUP):
            t = base + g * GROUP + n
            for k in range(2):
                outw[pl.ds(oslots[k, t] * 2, 2), :] = fin[32 * k + 2 * n : 32 * k + 2 * n + 2, :]
        return 0

    lax.fori_loop(0, HALF // GROUP, group, 0)
    for o in range(NKET):
        for b in range(CAPK // 16):
            r = o * CAPK + b * 16
            for k in range(2):
                out[o, b * 16 : b * 16 + 16, 128 * k : 128 * k + 128] = outw[
                    pl.ds(2 * r + k, 16, stride=2), :
                ].astype(BF16)
        out[o, CAPK:OUTROWS, :] = jnp.broadcast_to(places[half, o : o + 1, :], (16, 256)).astype(BF16)


def evaluate(half, tasks, slots, oslots, factors, fetched, places):
    return pl.pallas_call(
        functools.partial(eval_kernel, half),
        out_shape=jax.ShapeDtypeStruct((NKET, OUTROWS, 256), BF16),
        in_specs=[SM] * 3 + [VM] * 7,
        out_specs=VM,
        scratch_shapes=[
            pltpu.VMEM((NBLK * FUNCS, RANK), F32),
            pltpu.VMEM((2 * NBRA * CAPB, 128), F32),
            pltpu.VMEM((2 * NKET * CAPK, 128), F32),
            pltpu.VMEM((2 * GROUP, 128), F32),
            pltpu.VMEM((256, 256), BF16),
            pltpu.VMEM((256, 128), BF16),
            pltpu.VMEM((256, 256), BF16),
            pltpu.VMEM((4 * GROUP, 128), F32),
        ],
        compiler_params=PARAMS,
    )(tasks, slots, oslots, factors, fetched, places, *constants())


SUMS = 4


def scatter_kernel(first, second, out, wide, where_v, where_s, sem, *accs):
    def clear(k, _):
        for u in range(4):
            r = pl.multiple_of((k * 4 + u) * 8, 8)
            for acc in accs:
                acc[pl.ds(r, 8), :] = jnp.zeros((8, 128), F32)
        return 0

    lax.fori_loop(0, 2 * NB // 32, clear, 0)
    for h, src in enumerate((first, second)):
        for o in range(NKET):
            at = h * NKET + o
            row = src[o, CAPK : CAPK + 16, :].astype(F32)
            pos = (row[0:1, 0:128] * 64.0 + row[0:1, 128:256]).astype(I32) - 1
            where_v[at : at + 1, :] = jnp.where(pos < 0, NB, pos)
            for b in range(CAPK // 16):
                r = at * CAPK + b * 16
                v = src[o, b * 16 : b * 16 + 16, :].astype(F32)
                wide[pl.ds(2 * r, 16, stride=2), :] = v[:, :128]
                wide[pl.ds(2 * r + 1, 16, stride=2), :] = v[:, 128:]
    copy = pltpu.make_async_copy(where_v, where_s, sem)
    copy.start()
    copy.wait()
    per = 2 * NKET // SUMS

    def source(s, _):
        def step(k, _):
            for u in range(8):
                p = k * 8 + u
                for q, acc in enumerate(accs):
                    at = q * per + s
                    r = where_s[at, p]
                    acc[pl.ds(2 * r, 2), :] += wide[pl.ds((at * CAPK + p) * 2, 2), :]
            return 0

        lax.fori_loop(0, CAPK // 8, step, 0)
        return 0

    lax.fori_loop(0, per, source, 0)

    def total(k, _):
        for u in range(4):
            r = pl.multiple_of((k * 4 + u) * 8, 8)
            v = accs[0][pl.ds(r, 8), :]
            for acc in accs[1:]:
                v = v + acc[pl.ds(r, 8), :]
            out[pl.ds(r, 8), :] = v
        return 0

    lax.fori_loop(0, 2 * NB // 32, total, 0)


def scatter(first, second):
    return pl.pallas_call(
        scatter_kernel,
        out_shape=jax.ShapeDtypeStruct((2 * NB, 128), F32),
        in_specs=[VM, VM],
        out_specs=VM,
        scratch_shapes=[
            pltpu.VMEM((4 * NKET * CAPK, 128), F32),
            pltpu.VMEM((2 * NKET, 128), I32),
            pltpu.SMEM((2 * NKET, 128), I32),
            pltpu.SemaphoreType.DMA,
        ]
        + [pltpu.VMEM((2 * NB + 8, 128), F32)] * SUMS,
        compiler_params=PARAMS,
    )(first, second)


def exchange(x, axis):
    return lax.all_to_all(x, axis, split_axis=0, concat_axis=0, tiled=True)


def body(quartet_tasks, factors, density):
    tasks = quartet_tasks.reshape(TASKS, 4).T
    dens = density.reshape(NB, BSZ)
    ids, slots, oslots, places = prep(tasks)
    asked = exchange(ids, "bra")
    fetched = []
    for h in range(2):
        blocks = gather(h, asked, dens)
        fetched.append(exchange(blocks.reshape(NBRA, CAPB, BSZ), "bra").reshape(NBRA * CAPB, BSZ))
    arrived = []
    for h in range(2):
        parts = evaluate(h, tasks, slots, oslots, factors, fetched[h], places)
        arrived.append(exchange(parts, "ket"))
    fock = scatter(arrived[0], arrived[1])
    return fock.reshape(ROWB, COLB, 1, BSZ)


def solution(mesh):
    placed = (P("bra", "ket", None, None), P(), P("bra", None, "ket", None))
    return jax.shard_map(
        body, mesh=mesh, in_specs=placed, out_specs=P("bra", None, "ket", None), check_vma=False
    )
```

```python
import functools

import jax
import jax.numpy as jnp
import numpy as np
from jax import lax
from jax.experimental import pallas as pl
from jax.experimental.pallas import tpu as pltpu
from jax.sharding import PartitionSpec as P

F32, BF16, I32 = jnp.float32, jnp.bfloat16, jnp.int32
FUNCS, RANK, BSZ = 16, 128, 256
NBLK, ROWB, COLB = 768, 48, 96
NBRA, NKET, TASKS = 16, 8, 512
HALF, CAPB, CAPK = 256, 96, 80
OUTROWS = 96
GROUP = 16
PAIR = 4
AHEAD = 8
NB = ROWB * COLB
VM = pl.BlockSpec(memory_space=pltpu.VMEM)
SM = pl.BlockSpec(memory_space=pltpu.SMEM)
PARAMS = pltpu.CompilerParams(vmem_limit_bytes=60 * 1024 * 1024)


def iota(shape, dim):
    return lax.broadcasted_iota(I32, shape, dim)


def nt_dot(a, b):
    return lax.dot_general(a, b, (((1,), (1,)), ((), ())), preferred_element_type=F32)


def ranks(owners, count, upper, carry):
    marks = (iota((count, HALF), 0) == owners).astype(F32)
    before = jnp.dot(marks.astype(BF16), upper, preferred_element_type=F32) + carry
    place = jnp.sum(before * marks, axis=0, keepdims=True).astype(I32)
    return marks, place, carry + jnp.sum(marks, axis=1, keepdims=True)


def table(marks, place, value, width):
    at = (iota((width, HALF), 0) == place).astype(BF16)
    high = (value // 64).astype(F32)
    low = (value % 64).astype(F32)
    return nt_dot((marks * high).astype(BF16), at), nt_dot((marks * low).astype(BF16), at)


def prep_kernel(tasks, ids, slots, oslots, places):
    upper = (iota((HALF, HALF), 0) < iota((HALF, HALF), 1)).astype(BF16)
    for h in range(2):
        i, j, c, d = (tasks[r : r + 1, h * HALF : (h + 1) * HALF] for r in range(4))
        carry = jnp.zeros((NBRA, 1), F32)
        high = low = 0.0
        for k, s in enumerate((c, j)):
            own = s // ROWB
            marks, place, carry = ranks(own, NBRA, upper, carry)
            slots[k : k + 1, h * HALF : (h + 1) * HALF] = own * CAPB + place
            a, b = table(marks, place, (s % ROWB) * COLB + d // NKET, 128)
            high, low = high + a, low + b
        got = (high * 64.0 + low).astype(I32)
        ids[:, h * 128 : (h + 1) * 128] = jnp.where(iota((NBRA, 128), 1) < CAPB, got, carry.astype(I32))
        carry = jnp.zeros((NKET, 1), F32)
        high = low = 0.0
        for k, s in enumerate((j, c)):
            own = s % NKET
            marks, place, carry = ranks(own, NKET, upper, carry)
            oslots[k : k + 1, h * HALF : (h + 1) * HALF] = own * CAPK + place
            a, b = table(marks, place, (i % ROWB) * COLB + s // NKET + 1, 128)
            high, low = high + a, low + b
        places[h, :, 0:128] = high
        places[h, :, 128:256] = low


def prep(tasks):
    return pl.pallas_call(
        prep_kernel,
        out_shape=(
            jax.ShapeDtypeStruct((NBRA, 256), I32),
            jax.ShapeDtypeStruct((2, TASKS), I32),
            jax.ShapeDtypeStruct((2, TASKS), I32),
            jax.ShapeDtypeStruct((2, NKET, 256), F32),
        ),
        in_specs=[VM],
        out_specs=(VM,) * 4,
        compiler_params=PARAMS,
    )(tasks)


def spread(src, dst, rows):
    def step(k, _):
        for u in range(4):
            r = pl.multiple_of(k * 64 + u * 16, 16)
            v = src[pl.ds(r, 16), :].astype(F32)
            dst[pl.ds(2 * r, 16, stride=2), :] = v[:, :128]
            dst[pl.ds(2 * r + 1, 16, stride=2), :] = v[:, 128:]
        return 0

    lax.fori_loop(0, rows // 64, step, 0)


def gather_kernel(half, ids, dens, out, wide, got):
    spread(dens, wide, NB)

    for s in range(NBRA):
        count = ids[s, half * 128 + CAPB]

        def step(k, _):
            for u in range(16):
                r = ids[s, half * 128 + u + k * 16]
                got[pl.ds(pl.multiple_of(k * 32, 32) + (s * CAPB + u) * 2, 2), :] = wide[pl.ds(r * 2, 2), :]
            return 0

        lax.fori_loop(0, (count + 15) >> 4, step, 0)

    def pack(k, _):
        for u in range(4):
            r = pl.multiple_of(k * 64 + u * 16, 16)
            out[pl.ds(r, 16), 0:128] = got[pl.ds(2 * r, 16, stride=2), :].astype(BF16)
            out[pl.ds(r, 16), 128:256] = got[pl.ds(2 * r + 1, 16, stride=2), :].astype(BF16)
        return 0

    lax.fori_loop(0, NBRA * CAPB // 64, pack, 0)


def gather(half, ids, dens):
    return pl.pallas_call(
        functools.partial(gather_kernel, half),
        out_shape=jax.ShapeDtypeStruct((NBRA * CAPB, 256), BF16),
        in_specs=[SM, VM],
        out_specs=VM,
        scratch_shapes=[pltpu.VMEM((2 * NB, 128), F32), pltpu.VMEM((2 * NBRA * CAPB, 128), F32)],
        compiler_params=PARAMS,
    )(ids, dens)


def constants():
    r = np.arange(256)
    lane = np.arange(128)
    spread_b = r[:, None] // 16 == lane[None, :] % 16
    sum_f = np.arange(16)[:, None] == r[None, :] // 16
    sum_b = r[:, None] // 16 == r[None, :] // 16
    swap = r[None, :] == (r[:, None] % 16) * 16 + r[:, None] // 16
    keep_f = np.arange(16)[:, None] == lane[None, :] % 16
    return [jnp.asarray(x, BF16) for x in (spread_b, sum_f, sum_b, swap)] + [jnp.asarray(keep_f, F32)]


def eval_kernel(
    half, tasks, slots, oslots, fac, fetched, places, spread_b, sum_f, sum_b, swap, keep_f, out,
    rows, wide, outw, cd, jd, dsp, part, fin,
):
    base = half * HALF

    def widen(k, _):
        for u in range(8):
            rows[pl.ds(pl.multiple_of((k * 8 + u) * 16, 16), 16), :] = fac[k * 8 + u].astype(F32)
        return 0

    lax.fori_loop(0, NBLK // 8, widen, 0)
    spread(fetched, wide, NBRA * CAPB)
    keep = keep_f[...]

    def pairs(x, y):
        fy = fac[y]
        return jnp.concatenate(
            [
                jnp.broadcast_to(rows[pl.ds(x * FUNCS + a, 1), :], (FUNCS, RANK)).astype(BF16) * fy
                for a in range(FUNCS)
            ],
            axis=0,
        )

    def group(g, _):
        for n in range(GROUP):
            t = base + g * GROUP + n
            cd[2 * n : 2 * n + 2, :] = wide[pl.ds(slots[0, t] * 2, 2), :]
            block = wide[pl.ds(slots[1, t] * 2, 2), :]
            jd[n * 16 : n * 16 + 16, 0:128] = (jnp.broadcast_to(block[0:1], (16, 128)) * keep).astype(BF16)
            jd[n * 16 : n * 16 + 16, 128:256] = (jnp.broadcast_to(block[1:2], (16, 128)) * keep).astype(BF16)
        dsp[...] = jnp.dot(jd[...], spread_b[...], preferred_element_type=F32)
        dcd = jnp.concatenate([cd[pl.ds(0, 16, stride=2), :], cd[pl.ds(1, 16, stride=2), :]], axis=1).astype(BF16)
        dcd = jnp.dot(dcd, swap[...], preferred_element_type=F32).astype(BF16)
        acc = jnp.zeros((GROUP, BSZ), F32)
        def start(n):
            t = base + g * GROUP + n
            bra = pairs(tasks[0, t], tasks[1, t])
            ket = pairs(tasks[3, t], tasks[2, t])
            return nt_dot(ket, bra)

        raws = {n: start(n) for n in range(AHEAD)}
        for n0 in range(0, GROUP, PAIR):
            for n in range(n0 + AHEAD, min(n0 + AHEAD + PAIR, GROUP)):
                raws[n] = start(n)
            for n in range(n0, n0 + PAIR):
                raw = raws.pop(n).astype(BF16)
                tile = raw * lax.rsqrt(raw * raw + BF16(1.0))
                coul = jnp.dot(dcd, tile, preferred_element_type=F32)
                acc = jnp.where(iota((GROUP, BSZ), 0) == n, coul, acc)
                terms = []
                for f in range(16):
                    dd = jnp.broadcast_to(dsp[n * 16 + f : n * 16 + f + 1, :], (16, 128)).astype(BF16)
                    dd = jnp.concatenate([dd, dd], axis=1)
                    terms.append(tile[16 * f : 16 * f + 16, :] * dd)
                while len(terms) > 1:
                    terms = [x + y for x, y in zip(terms[0::2], terms[1::2])]
                part[n * 16 : n * 16 + 16, :] = terms[0]
        full = jnp.dot(part[...], sum_b[...], preferred_element_type=F32)
        full = jnp.where((iota((256, 256), 0) % 16) == (iota((256, 256), 1) % 16), full, 0.0)
        exch = jnp.dot(sum_f[...], full.astype(BF16), preferred_element_type=F32) * (-0.5 * 0.0625)
        acc = acc * 0.0625
        for k, v in enumerate((acc, exch)):
            fin[pl.ds(32 * k, 16, stride=2), :] = v[:, :128]
            fin[pl.ds(32 * k + 1, 16, stride=2), :] = v[:, 128:]
        for n in range(GROUP):
            t = base + g * GROUP + n
            for k in range(2):
                outw[pl.ds(oslots[k, t] * 2, 2), :] = fin[32 * k + 2 * n : 32 * k + 2 * n + 2, :]
        return 0

    lax.fori_loop(0, HALF // GROUP, group, 0)
    for o in range(NKET):
        for b in range(CAPK // 16):
            r = o * CAPK + b * 16
            for k in range(2):
                out[o, b * 16 : b * 16 + 16, 128 * k : 128 * k + 128] = outw[
                    pl.ds(2 * r + k, 16, stride=2), :
                ].astype(BF16)
        out[o, CAPK:OUTROWS, :] = jnp.broadcast_to(places[half, o : o + 1, :], (16, 256)).astype(BF16)


def evaluate(half, tasks, slots, oslots, factors, fetched, places):
    return pl.pallas_call(
        functools.partial(eval_kernel, half),
        out_shape=jax.ShapeDtypeStruct((NKET, OUTROWS, 256), BF16),
        in_specs=[SM] * 3 + [VM] * 8,
        out_specs=VM,
        scratch_shapes=[
            pltpu.VMEM((NBLK * FUNCS, RANK), F32),
            pltpu.VMEM((2 * NBRA * CAPB, 128), F32),
            pltpu.VMEM((2 * NKET * CAPK, 128), F32),
            pltpu.VMEM((2 * GROUP, 128), F32),
            pltpu.VMEM((256, 256), BF16),
            pltpu.VMEM((256, 128), F32),
            pltpu.VMEM((256, 256), BF16),
            pltpu.VMEM((4 * GROUP, 128), F32),
        ],
        compiler_params=PARAMS,
    )(tasks, slots, oslots, factors, fetched, places, *constants())


SUMS = 4


def scatter_kernel(first, second, out, wide, where_v, where_s, sem, *accs):
    def clear(k, _):
        for u in range(16):
            r = pl.multiple_of((k * 16 + u) * 8, 8)
            for acc in accs:
                acc[pl.ds(r, 8), :] = jnp.zeros((8, 128), F32)
        return 0

    lax.fori_loop(0, 2 * NB // 128, clear, 0)
    for h, src in enumerate((first, second)):
        for o in range(NKET):
            at = h * NKET + o
            row = src[o, CAPK : CAPK + 16, :].astype(F32)
            pos = (row[0:1, 0:128] * 64.0 + row[0:1, 128:256]).astype(I32) - 1
            where_v[at : at + 1, :] = jnp.where(pos < 0, NB, pos)
            for b in range(CAPK // 16):
                r = at * CAPK + b * 16
                v = src[o, b * 16 : b * 16 + 16, :].astype(F32)
                wide[pl.ds(2 * r, 16, stride=2), :] = v[:, :128]
                wide[pl.ds(2 * r + 1, 16, stride=2), :] = v[:, 128:]
    copy = pltpu.make_async_copy(where_v, where_s, sem)
    copy.start()
    copy.wait()
    per = 2 * NKET // SUMS

    def add(k, _):
        for s in range(per):
            for u in range(8):
                for q, acc in enumerate(accs):
                    at = q * per + s
                    r = where_s[at, u + k * 8]
                    acc[pl.ds(2 * r, 2), :] += wide[pl.ds(pl.multiple_of(k * 16, 16) + (at * CAPK + u) * 2, 2), :]
        return 0

    lax.fori_loop(0, CAPK // 8, add, 0)

    def total(k, _):
        for u in range(16):
            r = pl.multiple_of((k * 16 + u) * 8, 8)
            v = accs[0][pl.ds(r, 8), :]
            for acc in accs[1:]:
                v = v + acc[pl.ds(r, 8), :]
            out[pl.ds(r, 8), :] = v
        return 0

    lax.fori_loop(0, 2 * NB // 128, total, 0)


def scatter(first, second):
    return pl.pallas_call(
        scatter_kernel,
        out_shape=jax.ShapeDtypeStruct((2 * NB, 128), F32),
        in_specs=[VM, VM],
        out_specs=VM,
        scratch_shapes=[
            pltpu.VMEM((4 * NKET * CAPK, 128), F32),
            pltpu.VMEM((2 * NKET, 128), I32),
            pltpu.SMEM((2 * NKET, 128), I32),
            pltpu.SemaphoreType.DMA,
        ]
        + [pltpu.VMEM((2 * NB + 8, 128), F32)] * SUMS,
        compiler_params=PARAMS,
    )(first, second)


def exchange(x, axis):
    return lax.all_to_all(x, axis, split_axis=0, concat_axis=0, tiled=True)


def body(quartet_tasks, factors, density):
    tasks = quartet_tasks.reshape(TASKS, 4).T
    dens = density.reshape(NB, BSZ)
    ids, slots, oslots, places = prep(tasks)
    asked = exchange(ids, "bra")
    fetched = []
    for h in range(2):
        blocks = gather(h, asked, dens)
        fetched.append(exchange(blocks.reshape(NBRA, CAPB, BSZ), "bra").reshape(NBRA * CAPB, BSZ))
    arrived = []
    for h in range(2):
        parts = evaluate(h, tasks, slots, oslots, factors, fetched[h], places)
        arrived.append(exchange(parts, "ket"))
    fock = scatter(arrived[0], arrived[1])
    return fock.reshape(ROWB, COLB, 1, BSZ)


def solution(mesh):
    placed = (P("bra", "ket", None, None), P(), P("bra", None, "ket", None))
    return jax.shard_map(
        body, mesh=mesh, in_specs=placed, out_specs=P("bra", None, "ket", None), check_vma=False
    )
```

```python
import functools

import jax
import jax.numpy as jnp
import numpy as np
from jax import lax
from jax.experimental import pallas as pl
from jax.experimental.pallas import tpu as pltpu
from jax.sharding import PartitionSpec as P

F32, BF16, I32 = jnp.float32, jnp.bfloat16, jnp.int32
FUNCS, RANK, BSZ = 16, 128, 256
NBLK, ROWB, COLB = 768, 48, 96
NBRA, NKET, TASKS = 16, 8, 512
CHUNK, CAPB, CAPK = 256, 192, 160
OUTROWS = 176
GROUP, LAG, LATE, AT = 16, 4, 4, 4
GROUPS = TASKS // GROUP
SAVED = 8
FRESH = GROUPS - SAVED
STORED = SAVED * GROUP
NB = ROWB * COLB
VM = pl.BlockSpec(memory_space=pltpu.VMEM)
SM = pl.BlockSpec(memory_space=pltpu.SMEM)
PARAMS = pltpu.CompilerParams(vmem_limit_bytes=56 * 1024 * 1024)


def iota(shape, dim):
    return lax.broadcasted_iota(I32, shape, dim)


def nt_dot(a, b):
    return lax.dot_general(a, b, (((1,), (1,)), ((), ())), preferred_element_type=F32)


def ranks(owners, count, upper, carry):
    marks = (iota((count, CHUNK), 0) == owners).astype(F32)
    before = jnp.dot(marks.astype(BF16), upper, preferred_element_type=F32) + carry
    place = jnp.sum(before * marks, axis=0, keepdims=True).astype(I32)
    return marks, place, carry + jnp.sum(marks, axis=1, keepdims=True)


def table(marks, place, value):
    at = (iota((256, CHUNK), 0) == place).astype(BF16)
    high = (value >> 6).astype(F32)
    low = (value & 63).astype(F32)
    return nt_dot((marks * high).astype(BF16), at), nt_dot((marks * low).astype(BF16), at)


def prep_kernel(tasks, ids, slots, oslots, places):
    upper = (iota((CHUNK, CHUNK), 0) < iota((CHUNK, CHUNK), 1)).astype(BF16)
    carry = jnp.zeros((NBRA, 1), F32)
    ocarry = jnp.zeros((NKET, 1), F32)
    high = low = ohigh = olow = 0.0
    for h in range(TASKS // CHUNK):
        cols = slice(h * CHUNK, (h + 1) * CHUNK)
        i, j, c, d = (tasks[r : r + 1, cols] for r in range(4))
        for k, s in enumerate((c, j)):
            own = lax.div(s, ROWB)
            marks, place, carry = ranks(own, NBRA, upper, carry)
            slots[k : k + 1, cols] = own * CAPB + place
            a, b = table(marks, place, lax.rem(s, ROWB) * COLB + (d >> 3))
            high, low = high + a, low + b
        for k, s in enumerate((j, c)):
            own = s & (NKET - 1)
            marks, place, ocarry = ranks(own, NKET, upper, ocarry)
            oslots[k : k + 1, cols] = own * CAPK + place
            a, b = table(marks, place, lax.rem(i, ROWB) * COLB + (s >> 3) + 1)
            ohigh, olow = ohigh + a, olow + b
    got = (high * 64.0 + low).astype(I32)
    ids[...] = jnp.where(iota((NBRA, 256), 1) < CAPB, got, carry.astype(I32))
    places[0] = ohigh
    places[1] = olow


def prep(tasks):
    return pl.pallas_call(
        prep_kernel,
        out_shape=(
            jax.ShapeDtypeStruct((NBRA, 256), I32),
            jax.ShapeDtypeStruct((2, TASKS), I32),
            jax.ShapeDtypeStruct((2, TASKS), I32),
            jax.ShapeDtypeStruct((2, NKET, 256), F32),
        ),
        in_specs=[VM],
        out_specs=(VM,) * 4,
        compiler_params=PARAMS,
    )(tasks)


def spread(src, dst, rows):
    def step(k, _):
        for u in range(4):
            r = pl.multiple_of(k * 64 + u * 16, 16)
            v = src[pl.ds(r, 16), :].astype(F32)
            dst[pl.ds(2 * r, 16, stride=2), :] = v[:, :128]
            dst[pl.ds(2 * r + 1, 16, stride=2), :] = v[:, 128:]
        return 0

    lax.fori_loop(0, rows // 64, step, 0)


def gather_kernel(ids, dens, out, wide, got):
    spread(dens, wide, NB)

    for s in range(NBRA):
        count = ids[s, CAPB]

        def step(k, _):
            for u in range(16):
                r = ids[s, u + k * 16]
                got[pl.ds(pl.multiple_of(k * 32, 32) + (s * CAPB + u) * 2, 2), :] = wide[pl.ds(r * 2, 2), :]
            return 0

        lax.fori_loop(0, (count + 15) >> 4, step, 0)

    def pack(k, _):
        for u in range(4):
            r = pl.multiple_of(k * 64 + u * 16, 16)
            out[pl.ds(r, 16), 0:128] = got[pl.ds(2 * r, 16, stride=2), :].astype(BF16)
            out[pl.ds(r, 16), 128:256] = got[pl.ds(2 * r + 1, 16, stride=2), :].astype(BF16)
        return 0

    lax.fori_loop(0, NBRA * CAPB // 64, pack, 0)


def gather(ids, dens):
    return pl.pallas_call(
        gather_kernel,
        out_shape=jax.ShapeDtypeStruct((NBRA * CAPB, 256), BF16),
        in_specs=[SM, VM],
        out_specs=VM,
        scratch_shapes=[pltpu.VMEM((2 * NB, 128), F32), pltpu.VMEM((2 * NBRA * CAPB, 128), F32)],
        compiler_params=PARAMS,
    )(ids, dens)


def constants():
    r = np.arange(256)
    lane = np.arange(128)
    spread_b = r[:, None] // 16 == lane[None, :] % 16
    sum_f = np.arange(16)[:, None] == r[None, :] // 16
    sum_b = r[:, None] // 16 == r[None, :] // 16
    swap = r[None, :] == (r[:, None] % 16) * 16 + r[:, None] // 16
    keep_f = np.arange(16)[:, None] == lane[None, :] % 16
    return [jnp.asarray(x, BF16) for x in (spread_b, sum_f, sum_b, swap)] + [jnp.asarray(keep_f, F32)]


def pairs(fac, rows, x, y):
    fy = fac[y]
    return jnp.concatenate(
        [
            jnp.broadcast_to(rows[pl.ds(x * FUNCS + a, 1), :], (FUNCS, RANK)).astype(BF16) * fy
            for a in range(FUNCS)
        ],
        axis=0,
    )


def start(tasks, fac, rows, t):
    bra = pairs(fac, rows, tasks[0, t], tasks[1, t])
    ket = pairs(fac, rows, tasks[3, t], tasks[2, t])
    return nt_dot(ket, bra)


def tile_of(raw):
    raw = raw.astype(BF16)
    return raw * lax.rsqrt(raw * raw + BF16(1.0))


def widen(fac, rows):
    def step(k, _):
        for u in range(16):
            rows[pl.ds(pl.multiple_of((k * 16 + u) * 16, 16), 16), :] = fac[k * 16 + u].astype(F32)
        return 0

    lax.fori_loop(0, NBLK // 16, step, 0)


UNROLL, LEAD = 16, 4


def tile_kernel(tasks, fac, after, tiles, rows, buf_a, buf_b, sem):
    widen(fac, rows)
    size = UNROLL * 256

    def copy(k, buf, which):
        return pltpu.make_async_copy(buf, tiles.at[pl.ds(pl.multiple_of(k * size, size), size)], sem.at[which])

    def step(m, _):
        for which, buf in enumerate((buf_a, buf_b)):
            k = 2 * m + which

            @pl.when(m > 0)
            def _():
                copy(k - 2, buf, which).wait()

            raws = {}
            for n in range(UNROLL + LEAD):
                if n < UNROLL:
                    raws[n] = start(tasks, fac, rows, TASKS - STORED + k * UNROLL + n)
                if n >= LEAD:
                    buf[(n - LEAD) * 256 : (n - LEAD) * 256 + 256, :] = tile_of(raws.pop(n - LEAD))
            copy(k, buf, which).start()
        return 0

    count = STORED // UNROLL
    lax.fori_loop(0, count // 2, step, 0)
    copy(count - 2, buf_a, 0).wait()
    copy(count - 1, buf_b, 1).wait()


def early_tiles(tasks, factors, after):
    return pl.pallas_call(
        tile_kernel,
        out_shape=pltpu.HBM((STORED * 256, 256), BF16),
        in_specs=[SM, VM, pl.BlockSpec(memory_space=pltpu.HBM)],
        out_specs=pl.BlockSpec(memory_space=pltpu.HBM),
        scratch_shapes=[
            pltpu.VMEM((NBLK * FUNCS, RANK), F32),
            pltpu.VMEM((UNROLL * 256, 256), BF16),
            pltpu.VMEM((UNROLL * 256, 256), BF16),
            pltpu.SemaphoreType.DMA((2,)),
        ],
        compiler_params=pltpu.CompilerParams(vmem_limit_bytes=24 * 1024 * 1024),
    )(tasks, factors, after)


def eval_kernel(
    tasks, slots, oslots, fac, saved, fetched, places, spread_b, sum_f, sum_b, swap, keep_f, out,
    rows, wide, outw, cd, jd, fin, stored, sem, *double,
):
    dsp, part, held, dcd, tiles = (double[k : k + 2] for k in range(0, 10, 2))

    def load(k):
        at = pl.ds(pl.multiple_of(k * (GROUP * 256), GROUP * 256), GROUP * 256)
        return pltpu.make_async_copy(saved.at[at], stored.at[at], sem.at[k])

    for k in range(SAVED):
        load(k).start()
    widen(fac, rows)
    spread(fetched, wide, NBRA * CAPB)
    keep = keep_f[...]

    def density(g, par):
        for n in range(GROUP):
            t = g * GROUP + n
            cd[2 * n : 2 * n + 2, :] = wide[pl.ds(slots[0, t] * 2, 2), :]
            block = wide[pl.ds(slots[1, t] * 2, 2), :]
            jd[n * 16 : n * 16 + 16, 0:128] = (jnp.broadcast_to(block[0:1], (16, 128)) * keep).astype(BF16)
            jd[n * 16 : n * 16 + 16, 128:256] = (jnp.broadcast_to(block[1:2], (16, 128)) * keep).astype(BF16)
        dsp[par][...] = jnp.dot(jd[...], spread_b[...], preferred_element_type=F32)
        both = jnp.concatenate([cd[pl.ds(0, 16, stride=2), :], cd[pl.ds(1, 16, stride=2), :]], axis=1).astype(BF16)
        dcd[par][...] = jnp.dot(both, swap[...], preferred_element_type=F32).astype(BF16)

    def deliver(g, par):
        full = jnp.dot(part[par][...], sum_b[...], preferred_element_type=F32)
        full = jnp.where((iota((256, 256), 0) & 15) == (iota((256, 256), 1) & 15), full, 0.0)
        exch = jnp.dot(sum_f[...], full.astype(BF16), preferred_element_type=F32) * (-0.5 * 0.0625)
        for k, v in enumerate((held[par][...] * 0.0625, exch)):
            fin[pl.ds(32 * k, 16, stride=2), :] = v[:, :128]
            fin[pl.ds(32 * k + 1, 16, stride=2), :] = v[:, 128:]
        for n in range(GROUP):
            t = g * GROUP + n
            for k in range(2):
                outw[pl.ds(oslots[k, t] * 2, 2), :] = fin[32 * k + 2 * n : 32 * k + 2 * n + 2, :]

    def stage(g, par, ahead=True, here=True, behind=True, blocks=True, ready=None):
        nxt = 1 - par
        raws = {}
        acc = jnp.zeros((GROUP, BSZ), F32)
        if here:
            coef = dcd[par][...]
        for s0 in range(0, GROUP + LAG, PAIR):
            for n in range(s0, s0 + PAIR):
                if ahead and n < GROUP:
                    raws[n] = start(tasks, fac, rows, (g + 1) * GROUP + n)
            if s0 == AT and behind:
                deliver(g - 1, nxt)
            if s0 == AT + PAIR and blocks:
                density(g + 1, nxt)
            for n in range(s0 - LAG, s0 - LAG + PAIR):
                if ahead and n >= 0:
                    tiles[nxt][n * 256 : n * 256 + 256, :] = tile_of(raws.pop(n))
            for n in range(s0 - LATE, s0 - LATE + PAIR):
                if here and 0 <= n < GROUP:
                    if ready is None:
                        tile = tiles[par][n * 256 : n * 256 + 256, :]
                    else:
                        tile = stored[pl.ds(pl.multiple_of(ready * (GROUP * 256), 256) + n * 256, 256), :]
                    coul = jnp.dot(coef, tile, preferred_element_type=F32)
                    acc = jnp.where(iota((GROUP, BSZ), 0) == n, coul, acc)
                    terms = []
                    for f in range(16):
                        dd = jnp.broadcast_to(dsp[par][n * 16 + f : n * 16 + f + 1, :], (16, 128)).astype(BF16)
                        dd = jnp.concatenate([dd, dd], axis=1)
                        terms.append(tile[16 * f : 16 * f + 16, :] * dd)
                    while len(terms) > 1:
                        terms = [x + y for x, y in zip(terms[0::2], terms[1::2])]
                    part[par][n * 16 : n * 16 + 16, :] = terms[0]
        if here:
            held[par][...] = acc

    stage(-1, 1, here=False, behind=False)
    stage(0, 0, behind=False)

    def step(m, _):
        stage(2 * m + 1, 1)
        stage(2 * m + 2, 0)
        return 0

    lax.fori_loop(0, (FRESH - 2) // 2, step, 0)
    stage(FRESH - 1, 1, ahead=False, blocks=SAVED > 0)
    if SAVED:

        def finish(m, _):
            for par in range(2):
                load(2 * m + par).wait()
                stage(FRESH + 2 * m + par, par, ahead=False, ready=2 * m + par)
            return 0

        lax.fori_loop(0, SAVED // 2 - 1, finish, 0)
        load(SAVED - 2).wait()
        stage(GROUPS - 2, 0, ahead=False, ready=SAVED - 2)
        load(SAVED - 1).wait()
        stage(GROUPS - 1, 1, ahead=False, blocks=False, ready=SAVED - 1)
    deliver(GROUPS - 1, 1)
    for o in range(NKET):
        for b in range(CAPK // 16):
            r = o * CAPK + b * 16
            for k in range(2):
                out[o, b * 16 : b * 16 + 16, 128 * k : 128 * k + 128] = outw[
                    pl.ds(2 * r + k, 16, stride=2), :
                ].astype(BF16)
        two = jnp.where(
            (iota((16, 256), 0) & 1) == 0,
            jnp.broadcast_to(places[0, o : o + 1, :], (16, 256)),
            jnp.broadcast_to(places[1, o : o + 1, :], (16, 256)),
        )
        out[o, CAPK:OUTROWS, :] = two.astype(BF16)


PAIR = 2


def evaluate(tasks, slots, oslots, factors, saved, fetched, places):
    return pl.pallas_call(
        eval_kernel,
        out_shape=jax.ShapeDtypeStruct((NKET, OUTROWS, 256), BF16),
        in_specs=[SM] * 3 + [VM, pl.BlockSpec(memory_space=pltpu.HBM)] + [VM] * 7,
        out_specs=VM,
        scratch_shapes=[
            pltpu.VMEM((NBLK * FUNCS, RANK), F32),
            pltpu.VMEM((2 * NBRA * CAPB, 128), F32),
            pltpu.VMEM((2 * NKET * CAPK, 128), F32),
            pltpu.VMEM((2 * GROUP, 128), F32),
            pltpu.VMEM((256, 256), BF16),
            pltpu.VMEM((4 * GROUP, 128), F32),
            pltpu.VMEM((max(STORED, 1) * 256, 256), BF16),
            pltpu.SemaphoreType.DMA((max(SAVED, 1),)),
        ]
        + [pltpu.VMEM((256, 128), F32)] * 2
        + [pltpu.VMEM((256, 256), BF16)] * 2
        + [pltpu.VMEM((GROUP, BSZ), F32)] * 2
        + [pltpu.VMEM((GROUP, BSZ), BF16)] * 2
        + [pltpu.VMEM((GROUP * 256, 256), BF16)] * 2,
        compiler_params=PARAMS,
    )(tasks, slots, oslots, factors, saved, fetched, places, *constants())


SUMS = 4


def scatter_kernel(blocks, out, wide, where_v, where_s, sem, out_sem, total, *accs):
    def clear(k, _):
        for u in range(16):
            r = pl.multiple_of((k * 16 + u) * 8, 8)
            for acc in accs:
                acc[pl.ds(r, 8), :] = jnp.zeros((8, 128), F32)
        return 0

    lax.fori_loop(0, 2 * NB // 128, clear, 0)
    for o in range(NKET):
        row = blocks[o, CAPK:OUTROWS, :].astype(F32)
        pos = (row[0:1] * 64.0 + row[1:2]).astype(I32) - 1
        where_v[o : o + 1, :] = jnp.where(pos < 0, NB, pos)
        for b in range(CAPK // 16):
            r = o * CAPK + b * 16
            v = blocks[o, b * 16 : b * 16 + 16, :].astype(F32)
            wide[pl.ds(2 * r, 16, stride=2), :] = v[:, :128]
            wide[pl.ds(2 * r + 1, 16, stride=2), :] = v[:, 128:]
    copy = pltpu.make_async_copy(where_v, where_s, sem)
    copy.start()
    copy.wait()
    per = NKET // SUMS

    def add(k, _):
        for s in range(per):
            for u in range(8):
                for q, acc in enumerate(accs):
                    at = q * per + s
                    r = where_s[at, u + k * 8]
                    acc[pl.ds(2 * r, 2), :] += wide[pl.ds(pl.multiple_of(k * 16, 16) + (at * CAPK + u) * 2, 2), :]
        return 0

    lax.fori_loop(0, CAPK // 8, add, 0)
    size = 2 * NB // PIECES
    copies = []
    for piece in range(PIECES):

        def gather_sums(k, _):
            for u in range(16):
                r = pl.multiple_of(piece * size + (k * 16 + u) * 8, 8)
                v = accs[0][pl.ds(r, 8), :]
                for acc in accs[1:]:
                    v = v + acc[pl.ds(r, 8), :]
                total[pl.ds(r, 8), :] = v
            return 0

        lax.fori_loop(0, size // 128, gather_sums, 0)
        part = pl.ds(piece * size, size)
        copies.append(pltpu.make_async_copy(total.at[part], out.at[part], out_sem.at[piece]))
        copies[-1].start()
    for copy in copies:
        copy.wait()


PIECES = 6


def scatter(blocks):
    return pl.pallas_call(
        scatter_kernel,
        out_shape=jax.ShapeDtypeStruct((2 * NB, 128), F32),
        in_specs=[VM],
        out_specs=pl.BlockSpec(memory_space=pl.ANY),
        scratch_shapes=[
            pltpu.VMEM((2 * NKET * CAPK, 128), F32),
            pltpu.VMEM((NKET, 256), I32),
            pltpu.SMEM((NKET, 256), I32),
            pltpu.SemaphoreType.DMA,
            pltpu.SemaphoreType.DMA((PIECES,)),
            pltpu.VMEM((2 * NB, 128), F32),
        ]
        + [pltpu.VMEM((2 * NB + 8, 128), F32)] * SUMS,
        compiler_params=PARAMS,
    )(blocks)


def exchange(x, axis):
    return lax.all_to_all(x, axis, split_axis=0, concat_axis=0, tiled=True)


def body(quartet_tasks, factors, density):
    tasks = quartet_tasks.reshape(TASKS, 4).T
    dens = density.reshape(NB, BSZ)
    ids, slots, oslots, places = prep(tasks)
    blocks = gather(exchange(ids, "bra"), dens).reshape(NBRA, CAPB, BSZ)
    fetched = exchange(blocks, "bra").reshape(NBRA * CAPB, BSZ)
    tiles = early_tiles(tasks, factors, pltpu.with_memory_space_constraint(blocks, pltpu.HBM))
    tiles = pltpu.with_memory_space_constraint(tiles, pltpu.HBM)
    parts = evaluate(tasks, slots, oslots, factors, tiles, fetched, places)
    fock = scatter(exchange(parts, "ket"))
    return fock.reshape(ROWB, COLB, 1, BSZ)


def solution(mesh):
    placed = (P("bra", "ket", None, None), P(), P("bra", None, "ket", None))
    return jax.shard_map(
        body, mesh=mesh, in_specs=placed, out_specs=P("bra", None, "ket", None), check_vma=False
    )
```

```python
import functools

import jax
import jax.numpy as jnp
import numpy as np
from jax import lax
from jax.experimental import pallas as pl
from jax.experimental.pallas import tpu as pltpu
from jax.sharding import PartitionSpec as P

F32, BF16, I32 = jnp.float32, jnp.bfloat16, jnp.int32
FUNCS, RANK, BSZ = 16, 128, 256
NBLK, ROWB, COLB = 768, 48, 96
NBRA, NKET, TASKS = 16, 8, 512
CHUNK, CAPB, CAPK = 256, 192, 160
OUTROWS = 176
GROUP, LAG, LATE, AT = 16, 4, 4, 4
GROUPS = TASKS // GROUP
SAVED = 14
FRESH = GROUPS - SAVED
STORED = SAVED * GROUP
NB = ROWB * COLB
VM = pl.BlockSpec(memory_space=pltpu.VMEM)
SM = pl.BlockSpec(memory_space=pltpu.SMEM)
PARAMS = pltpu.CompilerParams(vmem_limit_bytes=58 * 1024 * 1024)


def iota(shape, dim):
    return lax.broadcasted_iota(I32, shape, dim)


def nt_dot(a, b):
    return lax.dot_general(a, b, (((1,), (1,)), ((), ())), preferred_element_type=F32)


def ranks(owners, count, upper, carry):
    marks = (iota((count, CHUNK), 0) == owners).astype(F32)
    before = jnp.dot(marks.astype(BF16), upper, preferred_element_type=F32) + carry
    place = jnp.sum(before * marks, axis=0, keepdims=True).astype(I32)
    return marks, place, carry + jnp.sum(marks, axis=1, keepdims=True)


def table(marks, place, value):
    at = (iota((256, CHUNK), 0) == place).astype(BF16)
    high = (value >> 6).astype(F32)
    low = (value & 63).astype(F32)
    return nt_dot((marks * high).astype(BF16), at), nt_dot((marks * low).astype(BF16), at)


def ask_kernel(tasks, ids, slots):
    upper = (iota((CHUNK, CHUNK), 0) < iota((CHUNK, CHUNK), 1)).astype(BF16)
    carry = jnp.zeros((NBRA, 1), F32)
    high = low = 0.0
    for h in range(TASKS // CHUNK):
        cols = slice(h * CHUNK, (h + 1) * CHUNK)
        for k, s in enumerate((tasks[2:3, cols], tasks[1:2, cols])):
            own = lax.div(s, ROWB)
            marks, place, carry = ranks(own, NBRA, upper, carry)
            slots[k : k + 1, cols] = own * CAPB + place
            a, b = table(marks, place, lax.rem(s, ROWB) * COLB + (tasks[3:4, cols] >> 3))
            high, low = high + a, low + b
    got = (high * 64.0 + low).astype(I32)
    ids[...] = jnp.where(iota((NBRA, 256), 1) < CAPB, got, carry.astype(I32))


def send_kernel(tasks, after, oslots, places):
    upper = (iota((CHUNK, CHUNK), 0) < iota((CHUNK, CHUNK), 1)).astype(BF16)
    carry = jnp.zeros((NKET, 1), F32)
    high = low = 0.0
    for h in range(TASKS // CHUNK):
        cols = slice(h * CHUNK, (h + 1) * CHUNK)
        for k, s in enumerate((tasks[1:2, cols], tasks[2:3, cols])):
            own = s & (NKET - 1)
            marks, place, carry = ranks(own, NKET, upper, carry)
            oslots[k : k + 1, cols] = own * CAPK + place
            a, b = table(marks, place, lax.rem(tasks[0:1, cols], ROWB) * COLB + (s >> 3) + 1)
            high, low = high + a, low + b
    places[0] = high
    places[1] = low


SMALL = pltpu.CompilerParams(vmem_limit_bytes=16 * 1024 * 1024)
PAIRS = jax.ShapeDtypeStruct((2, TASKS), I32)


def ask(tasks):
    return pl.pallas_call(
        ask_kernel,
        out_shape=(jax.ShapeDtypeStruct((NBRA, 256), I32), PAIRS),
        in_specs=[VM],
        out_specs=(VM, VM),
        compiler_params=SMALL,
    )(tasks)


def send(tasks, after):
    return pl.pallas_call(
        send_kernel,
        out_shape=(PAIRS, jax.ShapeDtypeStruct((2, NKET, 256), F32)),
        in_specs=[VM, pl.BlockSpec(memory_space=pltpu.HBM)],
        out_specs=(VM, VM),
        compiler_params=SMALL,
    )(tasks, after)


def spread(src, dst, rows):
    def step(k, _):
        for u in range(4):
            r = pl.multiple_of(k * 64 + u * 16, 16)
            v = src[pl.ds(r, 16), :].astype(F32)
            dst[pl.ds(2 * r, 16, stride=2), :] = v[:, :128]
            dst[pl.ds(2 * r + 1, 16, stride=2), :] = v[:, 128:]
        return 0

    lax.fori_loop(0, rows // 64, step, 0)


def gather_kernel(ids, dens, out, wide, got):
    spread(dens, wide, NB)

    for s in range(NBRA):
        count = ids[s, CAPB]

        def step(k, _):
            for u in range(16):
                r = ids[s, u + k * 16]
                got[pl.ds(pl.multiple_of(k * 32, 32) + (s * CAPB + u) * 2, 2), :] = wide[pl.ds(r * 2, 2), :]
            return 0

        lax.fori_loop(0, (count + 15) >> 4, step, 0)

    def pack(k, _):
        for u in range(4):
            r = pl.multiple_of(k * 64 + u * 16, 16)
            out[pl.ds(r, 16), 0:128] = got[pl.ds(2 * r, 16, stride=2), :].astype(BF16)
            out[pl.ds(r, 16), 128:256] = got[pl.ds(2 * r + 1, 16, stride=2), :].astype(BF16)
        return 0

    lax.fori_loop(0, NBRA * CAPB // 64, pack, 0)


def gather(ids, dens):
    return pl.pallas_call(
        gather_kernel,
        out_shape=jax.ShapeDtypeStruct((NBRA * CAPB, 256), BF16),
        in_specs=[SM, VM],
        out_specs=VM,
        scratch_shapes=[pltpu.VMEM((2 * NB, 128), F32), pltpu.VMEM((2 * NBRA * CAPB, 128), F32)],
        compiler_params=SMALL,
    )(ids, dens)


def constants():
    r = np.arange(256)
    lane = np.arange(128)
    spread_b = r[:, None] // 16 == lane[None, :] % 16
    sum_f = np.arange(16)[:, None] == r[None, :] // 16
    sum_b = r[:, None] // 16 == r[None, :] // 16
    swap = r[None, :] == (r[:, None] % 16) * 16 + r[:, None] // 16
    keep_f = np.arange(16)[:, None] == lane[None, :] % 16
    return [jnp.asarray(x, BF16) for x in (spread_b, sum_f, sum_b, swap)] + [jnp.asarray(keep_f, F32)]


def pairs(fac, rows, x, y):
    fy = fac[y]
    return jnp.concatenate(
        [
            jnp.broadcast_to(rows[pl.ds(x * FUNCS + a, 1), :], (FUNCS, RANK)).astype(BF16) * fy
            for a in range(FUNCS)
        ],
        axis=0,
    )


def start(tasks, fac, rows, t):
    bra = pairs(fac, rows, tasks[0, t], tasks[1, t])
    ket = pairs(fac, rows, tasks[3, t], tasks[2, t])
    return nt_dot(ket, bra)


def tile_of(raw):
    raw = raw.astype(BF16)
    return raw * lax.rsqrt(raw * raw + BF16(1.0))


def widen(fac, rows):
    def step(k, _):
        for u in range(16):
            rows[pl.ds(pl.multiple_of((k * 16 + u) * 16, 16), 16), :] = fac[k * 16 + u].astype(F32)
        return 0

    lax.fori_loop(0, NBLK // 16, step, 0)


UNROLL, LEAD = 16, 4


def tile_kernel(tasks, fac, after, tiles, rows, buf_a, buf_b, sem):
    widen(fac, rows)
    size = UNROLL * 256

    def copy(k, buf, which):
        return pltpu.make_async_copy(buf, tiles.at[pl.ds(pl.multiple_of(k * size, size), size)], sem.at[which])

    def step(m, _):
        for which, buf in enumerate((buf_a, buf_b)):
            k = 2 * m + which

            @pl.when(m > 0)
            def _():
                copy(k - 2, buf, which).wait()

            raws = {}
            for n in range(UNROLL + LEAD):
                if n < UNROLL:
                    raws[n] = start(tasks, fac, rows, TASKS - STORED + k * UNROLL + n)
                if n >= LEAD:
                    buf[(n - LEAD) * 256 : (n - LEAD) * 256 + 256, :] = tile_of(raws.pop(n - LEAD))
            copy(k, buf, which).start()
        return 0

    count = STORED // UNROLL
    lax.fori_loop(0, count // 2, step, 0)
    copy(count - 2, buf_a, 0).wait()
    copy(count - 1, buf_b, 1).wait()


def early_tiles(tasks, factors, after):
    return pl.pallas_call(
        tile_kernel,
        out_shape=pltpu.HBM((STORED * 256, 256), BF16),
        in_specs=[SM, VM, pl.BlockSpec(memory_space=pltpu.HBM)],
        out_specs=pl.BlockSpec(memory_space=pltpu.HBM),
        scratch_shapes=[
            pltpu.VMEM((NBLK * FUNCS, RANK), F32),
            pltpu.VMEM((UNROLL * 256, 256), BF16),
            pltpu.VMEM((UNROLL * 256, 256), BF16),
            pltpu.SemaphoreType.DMA((2,)),
        ],
        compiler_params=pltpu.CompilerParams(vmem_limit_bytes=24 * 1024 * 1024),
    )(tasks, factors, after)


def eval_kernel(
    tasks, slots, oslots, fac, saved, fetched, places, spread_b, sum_f, sum_b, swap, keep_f, out,
    rows, wide, outw, cd, jd, fin, stored, sem, *double,
):
    dsp, part, held, dcd, tiles = (double[k : k + 2] for k in range(0, 10, 2))

    def load(k):
        at = pl.ds(pl.multiple_of(k * (GROUP * 256), GROUP * 256), GROUP * 256)
        return pltpu.make_async_copy(saved.at[at], stored.at[at], sem.at[k])

    for k in range(SAVED):
        load(k).start()
    widen(fac, rows)
    spread(fetched, wide, NBRA * CAPB)
    keep = keep_f[...]

    def density(g, par):
        for n in range(GROUP):
            t = g * GROUP + n
            cd[2 * n : 2 * n + 2, :] = wide[pl.ds(slots[0, t] * 2, 2), :]
            block = wide[pl.ds(slots[1, t] * 2, 2), :]
            jd[n * 16 : n * 16 + 16, 0:128] = (jnp.broadcast_to(block[0:1], (16, 128)) * keep).astype(BF16)
            jd[n * 16 : n * 16 + 16, 128:256] = (jnp.broadcast_to(block[1:2], (16, 128)) * keep).astype(BF16)
        dsp[par][...] = jnp.dot(jd[...], spread_b[...], preferred_element_type=F32)
        both = jnp.concatenate([cd[pl.ds(0, 16, stride=2), :], cd[pl.ds(1, 16, stride=2), :]], axis=1).astype(BF16)
        dcd[par][...] = jnp.dot(both, swap[...], preferred_element_type=F32).astype(BF16)

    def deliver(g, par):
        full = jnp.dot(part[par][...], sum_b[...], preferred_element_type=F32)
        full = jnp.where((iota((256, 256), 0) & 15) == (iota((256, 256), 1) & 15), full, 0.0)
        exch = jnp.dot(sum_f[...], full.astype(BF16), preferred_element_type=F32) * (-0.5 * 0.0625)
        for k, v in enumerate((held[par][...] * 0.0625, exch)):
            fin[pl.ds(32 * k, 16, stride=2), :] = v[:, :128]
            fin[pl.ds(32 * k + 1, 16, stride=2), :] = v[:, 128:]
        for n in range(GROUP):
            t = g * GROUP + n
            for k in range(2):
                outw[pl.ds(oslots[k, t] * 2, 2), :] = fin[32 * k + 2 * n : 32 * k + 2 * n + 2, :]

    def stage(g, par, ahead=True, here=True, behind=True, blocks=True, ready=None):
        nxt = 1 - par
        raws = {}
        acc = jnp.zeros((GROUP, BSZ), F32)
        if here:
            coef = dcd[par][...]
        for s0 in range(0, GROUP + LAG, PAIR):
            for n in range(s0, s0 + PAIR):
                if ahead and n < GROUP:
                    raws[n] = start(tasks, fac, rows, (g + 1) * GROUP + n)
            if s0 == AT and behind:
                deliver(g - 1, nxt)
            if s0 == AT + PAIR and blocks:
                density(g + 1, nxt)
            for n in range(s0 - LAG, s0 - LAG + PAIR):
                if ahead and n >= 0:
                    tiles[nxt][n * 256 : n * 256 + 256, :] = tile_of(raws.pop(n))
            for n in range(s0 - LATE, s0 - LATE + PAIR):
                if here and 0 <= n < GROUP:
                    if ready is None:
                        tile = tiles[par][n * 256 : n * 256 + 256, :]
                    else:
                        tile = stored[pl.ds(pl.multiple_of(ready * (GROUP * 256), 256) + n * 256, 256), :]
                    coul = jnp.dot(coef, tile, preferred_element_type=F32)
                    acc = jnp.where(iota((GROUP, BSZ), 0) == n, coul, acc)
                    terms = []
                    for f in range(16):
                        dd = jnp.broadcast_to(dsp[par][n * 16 + f : n * 16 + f + 1, :], (16, 128)).astype(BF16)
                        dd = jnp.concatenate([dd, dd], axis=1)
                        terms.append(tile[16 * f : 16 * f + 16, :] * dd)
                    while len(terms) > 1:
                        terms = [x + y for x, y in zip(terms[0::2], terms[1::2])]
                    part[par][n * 16 : n * 16 + 16, :] = terms[0]
        if here:
            held[par][...] = acc

    stage(-1, 1, here=False, behind=False)
    stage(0, 0, behind=False)

    def step(m, _):
        stage(2 * m + 1, 1)
        stage(2 * m + 2, 0)
        return 0

    lax.fori_loop(0, (FRESH - 2) // 2, step, 0)
    stage(FRESH - 1, 1, ahead=False, blocks=SAVED > 0)
    if SAVED:

        def finish(m, _):
            for par in range(2):
                load(2 * m + par).wait()
                stage(FRESH + 2 * m + par, par, ahead=False, ready=2 * m + par)
            return 0

        lax.fori_loop(0, SAVED // 2 - 1, finish, 0)
        load(SAVED - 2).wait()
        stage(GROUPS - 2, 0, ahead=False, ready=SAVED - 2)
        load(SAVED - 1).wait()
        stage(GROUPS - 1, 1, ahead=False, blocks=False, ready=SAVED - 1)
    deliver(GROUPS - 1, 1)
    for o in range(NKET):
        for b in range(CAPK // 16):
            r = o * CAPK + b * 16
            for k in range(2):
                out[o, b * 16 : b * 16 + 16, 128 * k : 128 * k + 128] = outw[
                    pl.ds(2 * r + k, 16, stride=2), :
                ].astype(BF16)
        two = jnp.where(
            (iota((16, 256), 0) & 1) == 0,
            jnp.broadcast_to(places[0, o : o + 1, :], (16, 256)),
            jnp.broadcast_to(places[1, o : o + 1, :], (16, 256)),
        )
        out[o, CAPK:OUTROWS, :] = two.astype(BF16)


PAIR = 2


def evaluate(tasks, slots, oslots, factors, saved, fetched, places):
    return pl.pallas_call(
        eval_kernel,
        out_shape=jax.ShapeDtypeStruct((NKET, OUTROWS, 256), BF16),
        in_specs=[SM] * 3 + [VM, pl.BlockSpec(memory_space=pltpu.HBM)] + [VM] * 7,
        out_specs=VM,
        scratch_shapes=[
            pltpu.VMEM((NBLK * FUNCS, RANK), F32),
            pltpu.VMEM((2 * NBRA * CAPB, 128), F32),
            pltpu.VMEM((2 * NKET * CAPK, 128), F32),
            pltpu.VMEM((2 * GROUP, 128), F32),
            pltpu.VMEM((256, 256), BF16),
            pltpu.VMEM((4 * GROUP, 128), F32),
            pltpu.VMEM((max(STORED, 1) * 256, 256), BF16),
            pltpu.SemaphoreType.DMA((max(SAVED, 1),)),
        ]
        + [pltpu.VMEM((256, 128), F32)] * 2
        + [pltpu.VMEM((256, 256), BF16)] * 2
        + [pltpu.VMEM((GROUP, BSZ), F32)] * 2
        + [pltpu.VMEM((GROUP, BSZ), BF16)] * 2
        + [pltpu.VMEM((GROUP * 256, 256), BF16)] * 2,
        compiler_params=PARAMS,
    )(tasks, slots, oslots, factors, saved, fetched, places, *constants())


SUMS = 4


def scatter_kernel(blocks, out, wide, where_v, where_s, sem, out_sem, total, *accs):
    def clear(k, _):
        for u in range(16):
            r = pl.multiple_of((k * 16 + u) * 8, 8)
            for acc in accs:
                acc[pl.ds(r, 8), :] = jnp.zeros((8, 128), F32)
        return 0

    lax.fori_loop(0, 2 * NB // 128, clear, 0)
    for o in range(NKET):
        row = blocks[o, CAPK:OUTROWS, :].astype(F32)
        pos = (row[0:1] * 64.0 + row[1:2]).astype(I32) - 1
        where_v[o : o + 1, :] = jnp.where(pos < 0, NB, pos)
        for b in range(CAPK // 16):
            r = o * CAPK + b * 16
            v = blocks[o, b * 16 : b * 16 + 16, :].astype(F32)
            wide[pl.ds(2 * r, 16, stride=2), :] = v[:, :128]
            wide[pl.ds(2 * r + 1, 16, stride=2), :] = v[:, 128:]
    copy = pltpu.make_async_copy(where_v, where_s, sem)
    copy.start()
    copy.wait()
    per = NKET // SUMS

    def add(k, _):
        for s in range(per):
            for u in range(8):
                for q, acc in enumerate(accs):
                    at = q * per + s
                    r = where_s[at, u + k * 8]
                    acc[pl.ds(2 * r, 2), :] += wide[pl.ds(pl.multiple_of(k * 16, 16) + (at * CAPK + u) * 2, 2), :]
        return 0

    lax.fori_loop(0, CAPK // 8, add, 0)
    size = 2 * NB // PIECES
    copies = []
    for piece in range(PIECES):

        def gather_sums(k, _):
            for u in range(16):
                r = pl.multiple_of(piece * size + (k * 16 + u) * 8, 8)
                v = accs[0][pl.ds(r, 8), :]
                for acc in accs[1:]:
                    v = v + acc[pl.ds(r, 8), :]
                total[pl.ds(r, 8), :] = v
            return 0

        lax.fori_loop(0, size // 128, gather_sums, 0)
        part = pl.ds(piece * size, size)
        copies.append(pltpu.make_async_copy(total.at[part], out.at[part], out_sem.at[piece]))
        copies[-1].start()
    for copy in copies:
        copy.wait()


PIECES = 6


def scatter(blocks):
    return pl.pallas_call(
        scatter_kernel,
        out_shape=jax.ShapeDtypeStruct((2 * NB, 128), F32),
        in_specs=[VM],
        out_specs=pl.BlockSpec(memory_space=pl.ANY),
        scratch_shapes=[
            pltpu.VMEM((2 * NKET * CAPK, 128), F32),
            pltpu.VMEM((NKET, 256), I32),
            pltpu.SMEM((NKET, 256), I32),
            pltpu.SemaphoreType.DMA,
            pltpu.SemaphoreType.DMA((PIECES,)),
            pltpu.VMEM((2 * NB, 128), F32),
        ]
        + [pltpu.VMEM((2 * NB + 8, 128), F32)] * SUMS,
        compiler_params=pltpu.CompilerParams(vmem_limit_bytes=32 * 1024 * 1024),
    )(blocks)


def exchange(x, axis):
    return lax.all_to_all(x, axis, split_axis=0, concat_axis=0, tiled=True)


def body(quartet_tasks, factors, density):
    tasks = quartet_tasks.reshape(TASKS, 4).T
    dens = density.reshape(NB, BSZ)
    ids, slots = ask(tasks)
    blocks = gather(exchange(ids, "bra"), dens).reshape(NBRA, CAPB, BSZ)
    fetched = exchange(blocks, "bra").reshape(NBRA * CAPB, BSZ)
    gathered = pltpu.with_memory_space_constraint(blocks, pltpu.HBM)
    oslots, places = send(tasks, gathered)
    saved = pltpu.with_memory_space_constraint(early_tiles(tasks, factors, gathered), pltpu.HBM)
    parts = evaluate(tasks, slots, oslots, factors, saved, fetched, places)
    fock = scatter(exchange(parts, "ket"))
    return fock.reshape(ROWB, COLB, 1, BSZ)


def solution(mesh):
    placed = (P("bra", "ket", None, None), P(), P("bra", None, "ket", None))
    return jax.shard_map(
        body, mesh=mesh, in_specs=placed, out_specs=P("bra", None, "ket", None), check_vma=False
    )
```
